512 devices in a mesh: row: 32 (over y_lo, z), col: 16 (over x, y_hi, core).
Axes of the slice: x: 4, y: 4 (y_hi: 2, y_lo: 2; y = y_hi * 2 + y_lo), z: 16, core: 2. Of those that a mesh axis runs over, the one named last changes fastest.
Arguments:
- anc_inverse: float32 [16384, 16384], P('row', 'col')
- panel: float32 [7680, 2560], P('row', 'col'), may hold values from -0.00390625 to 0.00390625
- local_rows: int32 [7680], P('row'), may hold values from -1 to 511, as said below
- inv_diag: float32 [2560, 2560], P('row', 'col')
Outputs:
- sigma_off: float32 [7680, 2560], P('row', 'col')
- sigma_diag: float32 [2560, 2560], P('row', 'col')
The draws below stay inside these ranges and needn't reach their ends.
Inputs may be any that keep to these rules, and one draw needn't show every extreme that they name: `local_rows`: each aligned block of 240 slots lists its live ancestor rows first, distinct and ascending, then -1 in the rest; every block has at least one live slot, some block is full and some block is at most half full.
All inputs are finite; a program needn't handle non-finite values.
Results may differ from the reference program's by a relative error of at most 0.000075.
Values sent between devices are 32-bit elements; how exact they have to be, the bound alone decides.
A program may use at most 64 MiB of HBM per device.

```python
import math
import jax
import jax.numpy as jnp
from jax import lax

NA = 16384
NJ = 2560
CAP = 240
ANC_ROWS = 512
SLOTS = 7680


def draw_anc_inverse(key, part):
    first_key, second_key = jax.random.split(key)
    noise = jax.random.normal(first_key, (NA, NA), jnp.float32)
    lift = 1.0 + jax.random.uniform(second_key, (NA,), jnp.float32)
    scale_off = 0.7071 * SLOTS / math.sqrt(NA)
    offdiag = (noise + noise.T) * scale_off
    diag_index = jnp.arange(NA)
    return offdiag.at[diag_index, diag_index].add(SLOTS * lift)


def draw_inv_diag(key, part):
    first_key, second_key = jax.random.split(key)
    noise = jax.random.normal(first_key, (NJ, NJ), jnp.float32)
    lift = 1.0 + jax.random.uniform(second_key, (NJ,), jnp.float32)
    diag_index = jnp.arange(NJ)
    return ((noise + noise.T) * 0.35).at[diag_index, diag_index].add(lift)


def draw_local_rows(key, part):
    blocks = SLOTS // CAP
    count_key, full_key, perm_key = jax.random.split(jax.random.fold_in(key, 7), 3)
    counts = jax.random.randint(count_key, (blocks,), CAP // 2, CAP + 1)
    full_block = jax.random.randint(full_key, (), 0, blocks)
    half_block = (full_block + 1) % blocks
    block_ids = jnp.arange(blocks)
    counts = jnp.where(block_ids == full_block, CAP, counts)
    counts = jnp.where(block_ids == half_block, CAP // 2, counts)
    perm_keys = jax.random.split(perm_key, blocks)
    perms = jax.vmap(lambda one_key: jax.random.permutation(one_key, ANC_ROWS))(perm_keys)
    first_vals = perms[:, :1]
    swapped = jnp.where(perms == ANC_ROWS - 1, first_vals, perms)
    swapped = swapped.at[:, 0].set(ANC_ROWS - 1)
    perms = jnp.where((block_ids == full_block)[:, None], swapped, perms)[:, :CAP]
    position = jnp.arange(CAP)
    live = position[None, :] < counts[:, None]
    chosen = jnp.sort(jnp.where(live, perms, ANC_ROWS + 1), axis=1)
    result = jnp.where(chosen > ANC_ROWS, -1, chosen)
    return result.reshape(-1).astype(jnp.int32)


def shard_levels(rng, extent, cuts, smallest, largest):
    loudness = 1.0
    for dim, parts in cuts:
        draws = jax.random.uniform(jax.random.fold_in(jax.random.fold_in(rng, 6), dim), (parts,), jnp.float32, smallest / len(cuts), largest / len(cuts))
        loudness = loudness * jnp.repeat(jnp.exp(draws), extent[dim] // parts).reshape((-1,) + (1,) * (len(extent) - 1 - dim))
    return loudness


def bell_draw(rng, dims, scale, reach, pieces=(), kind=jnp.bfloat16):
    factor_of = shard_levels(rng, dims, pieces, -0.22, 0.18) if pieces else 1.0
    drawn = jax.random.normal(rng, dims, jnp.float32) * scale * factor_of
    return jnp.minimum(jnp.maximum(drawn, -reach), reach).astype(kind)


def setup_inputs(seed: int = 0) -> dict:
    splits = jax.random.split(jax.random.key(seed), 5)
    anc_inverse = draw_anc_inverse(jax.random.fold_in(splits[4], 71), 0)
    panel = bell_draw(splits[1], (SLOTS, NJ), (2.0 * SLOTS ** -1), 0.00390625, ((0, 32), (1, 16)), jnp.float32)
    local_rows = draw_local_rows(jax.random.fold_in(splits[4], 71), 0)
    inv_diag = draw_inv_diag(jax.random.fold_in(splits[4], 71), 0)
    return dict(anc_inverse=anc_inverse, panel=panel, local_rows=local_rows, inv_diag=inv_diag)


def reference(anc_inverse, panel, local_rows, inv_diag):
    slot_count = local_rows.shape[0]
    block_of = jnp.arange(slot_count, dtype=jnp.int32) // CAP
    live = (local_rows >= 0).astype(jnp.float32)
    anc = (block_of * ANC_ROWS + jnp.maximum(local_rows, 0)).astype(jnp.int32)
    picked = jnp.take(anc_inverse, anc, axis=0)
    compact = jnp.take(picked, anc, axis=1) * live[:, None] * live[None, :]
    sigma_off = -jnp.dot(compact, panel, precision=lax.Precision.HIGHEST)
    sigma_diag = inv_diag - jnp.dot(panel.T, sigma_off, precision=lax.Precision.HIGHEST)
    return sigma_off, sigma_diag
```

```python
import functools

import jax
import jax.numpy as jnp
from jax import lax
from jax.experimental import pallas as pl
from jax.experimental.pallas import tpu as pltpu
from jax.sharding import PartitionSpec as P

MESH = pl.DeviceIdType.MESH
Z = 16
SLOTS = 28
F32 = jnp.float32
BF16 = jnp.bfloat16


def split(value):
    high = value.astype(BF16)
    return high, (value - high.astype(F32)).astype(BF16)


def dot_nt(a, b):
    return lax.dot_general(a, b, (((1,), (1,)), ((), ())), preferred_element_type=F32)


def dot3(a, b):
    return dot_nt(a[0], b[0]) + (dot_nt(a[0], b[1]) + dot_nt(a[1], b[0]))


def remote(src, dst, send, recv, device):
    return pltpu.make_async_remote_copy(
        src_ref=src, dst_ref=dst, send_sem=send, recv_sem=recv, device_id=device, device_id_type=MESH
    )


def panel_kernel(
    xt, rows, lst, so, tp,
    XR, LB, CB, CH, CL, PB, RB, SG, XZ,
    xs, xr, asend, ls, lr, cs, cr, ds, dr, ss, sr, zs, zr, local,
):
    r, c = lax.axis_index("row"), lax.axis_index("col")
    yl, z = lax.div(r, Z), lax.rem(r, Z)
    k, p = lax.rem(c, 2), lax.div(c, 2)
    core = (r, c + 1 - 2 * k)
    across = (lax.rem(r + Z, 2 * Z), c)

    def at_z(step):
        return (Z * yl + lax.rem(z + step + Z, Z), c)

    up, down = at_z(1), at_z(-1)

    barrier = pltpu.get_barrier_semaphore()
    me = Z * yl + c

    @pl.loop(1, 32)
    def _(o):
        there = lax.rem(me + o, 32)
        pl.semaphore_signal(
            barrier, inc=1, device_id=(Z * lax.div(there, Z) + z, lax.rem(there, Z)), device_id_type=MESH
        )

    for there in (up, down):
        pl.semaphore_signal(barrier, inc=1, device_id=there, device_id_type=MESH)
    pl.semaphore_wait(barrier, 33)

    far = jnp.where(yl == lax.div(p, 4), 0, 1)

    def list_place(jj):
        return lax.rem(z - lax.rem(4 * p + 2 * k + jj, Z) + Z, Z)

    def list_slot(jj):
        e = list_place(jj)
        return jnp.minimum(e, Z - e) + far

    for jj in range(2):

        @pl.when((list_place(jj) == 0) & (far == 0))
        def _():
            pltpu.make_async_copy(lst, LB.at[jj], lr.at[jj]).start()

    def list_sends(jj):
        e = list_place(jj)
        return (
            (remote(LB.at[jj], LB.at[jj], ls.at[jj, 0], lr.at[jj], across), (e == 0) & (far == 0)),
            (remote(LB.at[jj], LB.at[jj], ls.at[jj, 1], lr.at[jj], up), e < 8),
            (remote(LB.at[jj], LB.at[jj], ls.at[jj, 2], lr.at[jj], down), (e == 0) | (e > 9)),
        )

    def list_step(jj):
        pltpu.make_async_copy(lst, LB.at[jj], lr.at[jj]).wait()
        for copy, wanted in list_sends(jj):
            pl.when(wanted)(copy.start)

    to_p, to_j, half_w = lax.div(r, 4), lax.rem(r, 4), lax.rem(p - lax.div(r, 4) + 8, 8)

    def own_send(h):
        return remote(
            xt.at[h], XR.at[to_j, half_w], asend.at[h], xr.at[to_j, half_w], (Z * h + z, 2 * to_p + k)
        )

    def own_local(h):
        return (to_p == p) & (yl == h)

    for jj in range(2):

        @pl.when(list_slot(jj) == 0)
        def _():
            list_step(jj)

    for h in range(2):

        @pl.when(own_local(h))
        def _():
            pltpu.make_async_copy(xt.at[h], XR.at[to_j, half_w], xr.at[to_j, half_w]).start()

        @pl.when(jnp.logical_not(own_local(h)))
        def _():
            own_send(h).start()

    base = lax.rem(4 * p, Z)
    u = lax.rem(z - base + Z, Z)
    v = lax.rem(base + 3 - z + Z, Z)

    def ring(j, w, there):
        return remote(XR.at[j, w], XR.at[j, w], xs.at[j, w], xr.at[j, w], there)

    def forward(s, place, way, odd):
        low, late = jnp.minimum(place, 3), jnp.maximum(place - 3, 0)

        def step(t, j, d):
            w = 2 * lax.div(t, 4) + odd
            copy = ring(3 - j if odd else j, w, way)
            copy.wait_recv()
            pl.when(d < 15)(copy.start)

        t = jnp.maximum(s - late, 0)
        i = lax.rem(t, 4)

        @pl.when((s >= late) & (t < 16) & (i <= low))
        def _():
            step(t, low - i, late + i)

        t2 = jnp.maximum(s - 12, 0)
        i2 = lax.rem(t2, 4)

        @pl.when((s >= 12) & (t2 < 16) & (i2 > low))
        def _():
            step(t2, low - i2 + 4, 12 + i2)

    tile, tile_half = lax.rem(c, 8), lax.div(c, 8)

    def plane_send(o):
        there = lax.rem(c + o, 16)
        return remote(
            xt.at[:, lax.rem(there, 2)], XZ.at[yl, tile], zs.at[o], zr.at[yl, tile], (Z * tile_half + z, there)
        )

    plane_self = tile_half == yl

    @pl.when(plane_self)
    def _():
        pltpu.make_async_copy(xt.at[:, k], XZ.at[yl, tile], zr.at[yl, tile]).start()

    def c_core():
        return remote(CB.at[yl, k], CB.at[yl, k], cs.at[0], cr.at[0], core)

    def c_across():
        return remote(CB.at[yl, k], CB.at[yl, k], cs.at[1], cr.at[1], across)

    def c_relay():
        return remote(CB.at[1 - yl, k], CB.at[1 - yl, k], cs.at[2], cr.at[2], core)

    pick_slot = jnp.maximum(list_slot(0), list_slot(1)) + 1

    def pick():
        for jj in range(2):
            hit = lax.broadcasted_iota(jnp.int32, (512, 256), 0).astype(F32) == LB[jj, 0:1, :]
            hit = jnp.where(hit, 1.0, 0.0).astype(BF16)
            block = rows[:, 512 * jj : 512 * jj + 512]
            high, mid = split(block)
            rest = ((block - high.astype(F32)) - mid.astype(F32)).astype(BF16)
            parts = [jnp.dot(x, hit, preferred_element_type=F32) for x in (high, mid, rest)]
            CB[yl, k, jj] = parts[0] + (parts[1] + parts[2])
        c_across().start()
        c_core().start()

    @pl.loop(0, SLOTS)
    def _(s):
        for jj in range(2):

            @pl.when((s > 0) & (list_slot(jj) == s))
            def _():
                list_step(jj)

        forward(s, u, up, 0)
        forward(s, v, down, 1)

        @pl.when(s == pick_slot)
        def _():
            pick()

        @pl.when(s == pick_slot + 8)
        def _():
            c_across().wait_recv()
            c_relay().start()

        @pl.when((s >= 4) & (s < 20) & jnp.logical_not(plane_self & (s == 4)))
        def _():
            plane_send(s - 4).start()

    c_core().wait_recv()
    c_relay().wait_recv()
    for yb in range(2):
        for j in range(4):
            high, low = split(CB[yb, j // 2, j % 2])
            CH[yb, j], CL[yb, j] = high, low

    def peer(w):
        return remote(PB.at[w], RB.at[w], ds.at[w], dr.at[w], (r, 2 * lax.rem(p + w, 8) + k))

    @pl.loop(0, 8)
    def _(o):
        w = 7 - o
        pieces = [split(XR[j, w].reshape(80, 256)) for j in range(4)]
        for yb in range(2):
            total = jnp.zeros((80, 256), F32)
            for j in range(4):
                total = total + dot3(pieces[j], (CH[yb, j], CL[yb, j]))
            PB[w, :, 256 * yb : 256 * yb + 256] = total

        @pl.when(w > 0)
        def _():
            peer(w).start()

    total = PB[0]
    for w in range(1, 8):
        peer(w).wait_recv()
        total = total + RB[w]
    SG[k, yl] = -total

    def s_across():
        return remote(SG.at[k, yl], SG.at[k, yl], ss.at[0], sr.at[0], across)

    def s_core():
        return remote(SG.at[k, yl], SG.at[k, yl], ss.at[1], sr.at[1], core)

    def s_relay():
        return remote(SG.at[k, 1 - yl], SG.at[k, 1 - yl], ss.at[2], sr.at[2], core)

    s_across().start()
    s_core().start()
    s_across().wait_recv()
    s_relay().start()
    so[...] = SG[k, :, :, pl.ds(pl.multiple_of(256 * yl, 256), 256)]
    s_core().wait_recv()
    s_relay().wait_recv()

    for i in range(16):
        pltpu.make_async_copy(xt.at[:, 0], XZ.at[i // 8, i % 8], zr.at[i // 8, i % 8]).wait()
    sides = [split(SG[:, :, :, 256 * yb : 256 * yb + 256].reshape(320, 256)) for yb in range(2)]

    @pl.loop(0, 8)
    def _(t):
        total = jnp.zeros((80, 320), F32)
        for yb in range(2):
            total = total + dot3(split(XZ[yb, t].reshape(80, 256)), sides[yb])
        tp[pl.ds(2 * t, 2), :, 0:320] = total.reshape(2, 40, 320)

    for jj in range(2):
        for copy, wanted in list_sends(jj):
            pl.when(wanted)(copy.wait_send)
    for h in range(2):
        pl.when(jnp.logical_not(own_local(h)))(own_send(h).wait_send)

    @pl.loop(0, 16)
    def _(n):
        j, q = lax.div(n, 4), lax.rem(n, 4)
        pl.when(lax.rem(u - j + Z, Z) < 15)(ring(j, 2 * q, up).wait_send)
        pl.when(lax.rem(v - 3 + j + Z, Z) < 15)(ring(j, 2 * q + 1, down).wait_send)
        pl.when(jnp.logical_not(plane_self & (n == 0)))(plane_send(n).wait_send)

    for copy in (c_core(), c_across(), c_relay(), s_across(), s_core(), s_relay()):
        copy.wait_send()

    @pl.loop(1, 8)
    def _(w):
        peer(w).wait_send()


def fold_kernel(tp, inv, out, SU, RU, SD, RD, PX, su, ru, sd, rd, px):
    r, c = lax.axis_index("row"), lax.axis_index("col")
    yl, z, k = lax.div(r, Z), lax.rem(r, Z), lax.rem(c, 2)
    core = (r, c + 1 - 2 * k)

    def at_z(step):
        return (Z * yl + lax.rem(z + step + Z, Z), c)

    barrier = pltpu.get_barrier_semaphore()
    for there in (at_z(1), at_z(-1), core):
        pl.semaphore_signal(barrier, inc=1, device_id=there, device_id_type=MESH)
    pl.semaphore_wait(barrier, 3)

    def up(s):
        return remote(SU.at[s], RU.at[s], su.at[s], ru.at[s], at_z(1))

    def down(s):
        return remote(SD.at[s], RD.at[s], sd.at[s], rd.at[s], at_z(-1))

    for s in range(8):
        mine = tp[lax.rem(z + 8 - s, Z)]
        if s:
            up(s - 1).wait_recv()
            mine = mine + RU[s - 1]
        SU[s] = mine
        up(s).start()
        if s < 7:
            mine = tp[lax.rem(z + 9 + s, Z)]
            if s:
                down(s - 1).wait_recv()
                mine = mine + RD[s - 1]
            SD[s] = mine
            down(s).start()
    down(6).wait_recv()
    mine = tp[z] + RD[6]
    up(7).wait_recv()
    PX[0] = mine + RU[7]
    swap = remote(PX.at[0], PX.at[1], px.at[0], px.at[1], core)
    swap.start()
    swap.wait_recv()
    own, other = PX[0], PX[1]
    own = jnp.where(k == 0, own[:, 0:160], own[:, 160:320])
    other = jnp.where(k == 0, other[:, 0:160], other[:, 160:320])
    out[0:40, :] = inv[0:40, :] - jnp.where(k == 0, own, other)
    out[40:80, :] = inv[40:80, :] - jnp.where(k == 0, other, own)
    swap.wait_send()
    for s in range(8):
        up(s).wait_send()
        if s < 7:
            down(s).wait_send()


def shards(anc_inverse, panel, local_rows, inv_diag):
    ids = jnp.pad(local_rows, (0, 16), constant_values=-1)
    live = (ids >= 0).astype(F32)
    rows = jnp.take(anc_inverse, jnp.maximum(ids, 0), axis=0) * live[:, None]
    lst = jnp.broadcast_to(ids.astype(F32)[None, :], (8, 256))
    xt = jnp.pad(panel, ((0, 16), (0, 0))).T.reshape(2, 2, 40, 256)
    vmem = pl.BlockSpec(memory_space=pltpu.VMEM)
    dma = pltpu.SemaphoreType.DMA
    so, tp = pl.pallas_call(
        panel_kernel,
        out_shape=(
            jax.ShapeDtypeStruct((2, 80, 256), F32),
            jax.ShapeDtypeStruct((Z, 40, 384), F32),
        ),
        in_specs=[vmem] * 3,
        out_specs=(vmem, vmem),
        scratch_shapes=[
            pltpu.VMEM((4, 8, 2, 40, 256), F32),
            pltpu.VMEM((2, 8, 256), F32),
            pltpu.VMEM((2, 2, 2, 256, 256), F32),
            pltpu.VMEM((2, 4, 256, 256), BF16),
            pltpu.VMEM((2, 4, 256, 256), BF16),
            pltpu.VMEM((8, 80, 512), F32),
            pltpu.VMEM((8, 80, 512), F32),
            pltpu.VMEM((2, 2, 80, 512), F32),
            pltpu.VMEM((2, 8, 2, 40, 256), F32),
            dma((4, 8)), dma((4, 8)),
            dma((2,)),
            dma((2, 3)), dma((2,)),
            dma((3,)), dma((3,)),
            dma((8,)), dma((8,)),
            dma((3,)), dma((3,)),
            dma((16,)), dma((2, 8)),
            dma((2,)),
        ],
        compiler_params=pltpu.CompilerParams(collective_id=0, has_side_effects=True),
        name="panel_products",
    )(xt, rows, lst)
    sigma_diag = pl.pallas_call(
        fold_kernel,
        out_shape=jax.ShapeDtypeStruct(inv_diag.shape, F32),
        in_specs=[vmem] * 2,
        out_specs=vmem,
        scratch_shapes=[pltpu.VMEM((8, 40, 384), F32)] * 4
        + [pltpu.VMEM((2, 40, 384), F32)]
        + [dma((8,))] * 4
        + [dma((2,))],
        compiler_params=pltpu.CompilerParams(collective_id=1, has_side_effects=True),
        name="fold_over_rows",
    )(tp, inv_diag)
    sigma_off = so.reshape(160, 256)[:, :240].T
    return (sigma_off, sigma_diag)


def solution(mesh):
    placed = (P("row", "col"), P("row", "col"), P("row"), P("row", "col"))
    return jax.shard_map(
        shards,
        mesh=mesh,
        in_specs=placed,
        out_specs=(P("row", "col"), P("row", "col")),
        check_vma=False,
    )
```

```python
import functools

import jax
import jax.numpy as jnp
from jax import lax
from jax.experimental import pallas as pl
from jax.experimental.pallas import tpu as pltpu
from jax.sharding import PartitionSpec as P

MESH = pl.DeviceIdType.MESH
Z = 16
PARTS = 1
PIECE = 80 // PARTS
HOP = 1
C_RELAY = 6
C_READY = 9
GROUPS = max(8 * PARTS + 3 + 12 * HOP, 10 + C_READY + 7 * PARTS) + 2
F32 = jnp.float32
BF16 = jnp.bfloat16


def split(value):
    high = value.astype(BF16)
    return high, (value - high.astype(F32)).astype(BF16)


def dot_nt(a, b):
    return lax.dot_general(a, b, (((1,), (1,)), ((), ())), preferred_element_type=F32)


def dot3(a, b):
    return dot_nt(a[0], b[0]) + (dot_nt(a[0], b[1]) + dot_nt(a[1], b[0]))


def remote(src, dst, send, recv, device):
    return pltpu.make_async_remote_copy(
        src_ref=src, dst_ref=dst, send_sem=send, recv_sem=recv, device_id=device, device_id_type=MESH
    )


def panel_kernel(
    xt, rows, lst, so, tp,
    XR, LB, CB, CH, CL, PB, RB, SG, XZ,
    xs, xr, asend, ls, lr, cs, cr, ds, dr, ss, sr, zs, zr,
):
    r, c = lax.axis_index("row"), lax.axis_index("col")
    yl, z = lax.div(r, Z), lax.rem(r, Z)
    k, p = lax.rem(c, 2), lax.div(c, 2)
    core = (r, c + 1 - 2 * k)
    across = (lax.rem(r + Z, 2 * Z), c)

    def at_z(step):
        return (Z * yl + lax.rem(z + step + Z, Z), c)

    up, down = at_z(1), at_z(-1)

    barrier = pltpu.get_barrier_semaphore()
    me = Z * yl + c

    @pl.loop(1, 32)
    def _(o):
        there = lax.rem(me + o, 32)
        pl.semaphore_signal(
            barrier, inc=1, device_id=(Z * lax.div(there, Z) + z, lax.rem(there, Z)), device_id_type=MESH
        )

    for there in (up, down):
        pl.semaphore_signal(barrier, inc=1, device_id=there, device_id_type=MESH)
    pl.semaphore_wait(barrier, 33)

    far = jnp.where(yl == lax.div(p, 4), 0, 1)

    def list_place(jj):
        return lax.rem(z - lax.rem(4 * p + 2 * k + jj, Z) + Z, Z)

    def list_slot(jj):
        e = list_place(jj)
        return jnp.minimum(e, Z - e) + far

    for jj in range(2):

        @pl.when((list_place(jj) == 0) & (far == 0))
        def _():
            pltpu.make_async_copy(lst, LB.at[jj], lr.at[jj]).start()

    def list_sends(jj):
        e = list_place(jj)
        return (
            (remote(LB.at[jj], LB.at[jj], ls.at[jj, 0], lr.at[jj], across), (e == 0) & (far == 0)),
            (remote(LB.at[jj], LB.at[jj], ls.at[jj, 1], lr.at[jj], up), e < 8),
            (remote(LB.at[jj], LB.at[jj], ls.at[jj, 2], lr.at[jj], down), (e == 0) | (e > 9)),
        )

    def list_step(jj):
        pltpu.make_async_copy(lst, LB.at[jj], lr.at[jj]).wait()
        for copy, wanted in list_sends(jj):
            pl.when(wanted)(copy.start)

    to_p, to_j, half_w = lax.div(r, 4), lax.rem(r, 4), lax.rem(p - lax.div(r, 4) + 8, 8)

    def own_pair(h, part):
        there = XR.at[to_j, half_w, pl.ds(PIECE * part, PIECE)]
        return xt.at[h, pl.ds(PIECE * part, PIECE)], there, xr.at[to_j, PARTS * half_w + part]

    def own_send(h, part):
        src, dst, sem = own_pair(h, part)
        return remote(src, dst, asend.at[h, part], sem, (Z * h + z, 2 * to_p + k))

    def own_local(h):
        return (to_p == p) & (yl == h)

    for jj in range(2):

        @pl.when(list_slot(jj) == 0)
        def _():
            list_step(jj)

    for part in range(PARTS):
        for h in range(2):

            @pl.when(own_local(h))
            def _():
                pltpu.make_async_copy(*own_pair(h, part)).start()

            @pl.when(jnp.logical_not(own_local(h)))
            def _():
                own_send(h, part).start()

    base = lax.rem(4 * p, Z)
    place = jnp.where(k == 0, lax.rem(z - base + Z, Z), lax.rem(base + 3 - z + Z, Z))
    low, late = jnp.minimum(place, 3), jnp.maximum(place - 3, 0)
    onward = at_z(1 - 2 * k)

    def ring(j, n):
        w, part = lax.div(n, PARTS), lax.rem(n, PARTS)
        piece = XR.at[j, w, pl.ds(PIECE * part, PIECE)]
        return remote(piece, piece, xs.at[j, n], xr.at[j, n], onward)

    def behind(i):
        return jnp.where(i <= low, late, 12)

    def line_block(i):
        line = jnp.where(i <= low, low - i, low - i + 4)
        return jnp.where(k == 0, line, 3 - line)

    def forward(g, i):
        n = g - HOP * behind(i) - i

        @pl.when((n >= 0) & (n < 8 * PARTS))
        def _():
            copy = ring(line_block(i), jnp.maximum(n, 0))
            copy.wait_recv()
            pl.when(behind(i) + i < 15)(copy.start)

    tile, tile_half = lax.rem(c, 8), lax.div(c, 8)

    def plane_send(o):
        there = lax.rem(c + o, 16)
        return remote(
            xt.at[:, pl.ds(40 * lax.rem(there, 2), 40)], XZ.at[yl, tile], zs.at[o], zr.at[yl, tile], (Z * tile_half + z, there)
        )

    plane_self = tile_half == yl

    @pl.when(plane_self)
    def _():
        pltpu.make_async_copy(xt.at[:, pl.ds(40 * k, 40)], XZ.at[yl, tile], zr.at[yl, tile]).start()

    def c_core():
        return remote(CB.at[yl, k], CB.at[yl, k], cs.at[0], cr.at[0], core)

    def c_across():
        return remote(CB.at[yl, k], CB.at[yl, k], cs.at[1], cr.at[1], across)

    def c_relay():
        return remote(CB.at[1 - yl, k], CB.at[1 - yl, k], cs.at[2], cr.at[2], core)

    pick_slot = jnp.maximum(list_slot(0), list_slot(1)) + 1
    c_slot = pick_slot + C_READY

    def pick():
        for jj in range(2):
            hit = lax.broadcasted_iota(jnp.int32, (512, 256), 0).astype(F32) == LB[jj, 0:1, :]
            hit = jnp.where(hit, 1.0, 0.0).astype(BF16)
            block = rows[:, 512 * jj : 512 * jj + 512]
            high, mid = split(block)
            rest = ((block - high.astype(F32)) - mid.astype(F32)).astype(BF16)
            parts = [jnp.dot(x, hit, preferred_element_type=F32) for x in (high, mid, rest)]
            CB[yl, k, jj] = parts[0] + (parts[1] + parts[2])
        c_across().start()
        c_core().start()

    def c_arrived():
        c_core().wait_recv()
        c_relay().wait_recv()
        for yb in range(2):
            for j in range(4):
                high, low = split(CB[yb, j // 2, j % 2])
                CH[yb, j], CL[yb, j] = high, low

    def peer(w):
        return remote(PB.at[w], RB.at[w], ds.at[w], dr.at[w], (r, 2 * lax.rem(p + w, 8) + k))

    def multiply(w):
        pieces = [split(XR[j, w]) for j in range(4)]
        for yb in range(2):
            total = jnp.zeros((80, 256), F32)
            for j in range(4):
                total = total + dot3(pieces[j], (CH[yb, j], CL[yb, j]))
            PB[w, :, 256 * yb : 256 * yb + 256] = total

        @pl.when(w > 0)
        def _():
            peer(w).start()

    first_multiply = jnp.maximum(PARTS + 3 + HOP * behind(3), c_slot)

    @pl.loop(0, GROUPS)
    def _(g):
        for jj in range(2):

            @pl.when((g > 0) & (list_slot(jj) == g))
            def _():
                list_step(jj)

        for i in range(4):
            forward(g, i)

        pl.when(g == pick_slot)(pick)

        @pl.when(g == pick_slot + C_RELAY)
        def _():
            c_across().wait_recv()
            c_relay().start()

        @pl.when((g >= 1) & (g <= 16) & jnp.logical_not(plane_self & (g == 1)))
        def _():
            plane_send(g - 1).start()

        pl.when(g == c_slot)(c_arrived)
        ready = g - first_multiply

        @pl.when((ready >= 0) & (ready < 8 * PARTS) & (lax.rem(jnp.maximum(ready, 0), PARTS) == 0))
        def _():
            multiply(lax.div(ready, PARTS))

    total = PB[0]
    for w in range(1, 8):
        peer(w).wait_recv()
        total = total + RB[w]
    SG[k, yl] = -total

    def s_across():
        return remote(SG.at[k, yl], SG.at[k, yl], ss.at[0], sr.at[0], across)

    def s_core():
        return remote(SG.at[k, yl], SG.at[k, yl], ss.at[1], sr.at[1], core)

    def s_relay():
        return remote(SG.at[k, 1 - yl], SG.at[k, 1 - yl], ss.at[2], sr.at[2], core)

    s_across().start()
    s_core().start()
    s_across().wait_recv()
    s_relay().start()
    so[...] = SG[k, :, :, pl.ds(pl.multiple_of(256 * yl, 256), 256)]
    s_core().wait_recv()
    s_relay().wait_recv()

    for i in range(16):
        pltpu.make_async_copy(xt.at[:, pl.ds(0, 40)], XZ.at[i // 8, i % 8], zr.at[i // 8, i % 8]).wait()
    sides = [split(SG[:, :, :, 256 * yb : 256 * yb + 256].reshape(320, 256)) for yb in range(2)]

    @pl.loop(0, 8)
    def _(t):
        total = jnp.zeros((80, 320), F32)
        for yb in range(2):
            total = total + dot3(split(XZ[yb, t].reshape(80, 256)), sides[yb])
        tp[pl.ds(2 * t, 2), :, 0:320] = total.reshape(2, 40, 320)

    for jj in range(2):
        for copy, wanted in list_sends(jj):
            pl.when(wanted)(copy.wait_send)
    for h in range(2):
        for part in range(PARTS):
            pl.when(jnp.logical_not(own_local(h)))(own_send(h, part).wait_send)

    @pl.loop(0, 16)
    def _(n):
        pl.when(jnp.logical_not(plane_self & (n == 0)))(plane_send(n).wait_send)

    for i in range(4):

        @pl.when(behind(i) + i < 15)
        def _():
            @pl.loop(0, 8 * PARTS)
            def _(n):
                ring(line_block(i), n).wait_send()

    for copy in (c_core(), c_across(), c_relay(), s_across(), s_core(), s_relay()):
        copy.wait_send()

    @pl.loop(1, 8)
    def _(w):
        peer(w).wait_send()


def fold_kernel(tp, inv, out, SU, RU, SD, RD, PX, su, ru, sd, rd, px):
    r, c = lax.axis_index("row"), lax.axis_index("col")
    yl, z, k = lax.div(r, Z), lax.rem(r, Z), lax.rem(c, 2)
    core = (r, c + 1 - 2 * k)

    def at_z(step):
        return (Z * yl + lax.rem(z + step + Z, Z), c)

    barrier = pltpu.get_barrier_semaphore()
    for there in (at_z(1), at_z(-1), core):
        pl.semaphore_signal(barrier, inc=1, device_id=there, device_id_type=MESH)
    pl.semaphore_wait(barrier, 3)

    def up(s):
        return remote(SU.at[s], RU.at[s], su.at[s], ru.at[s], at_z(1))

    def down(s):
        return remote(SD.at[s], RD.at[s], sd.at[s], rd.at[s], at_z(-1))

    for s in range(8):
        mine = tp[lax.rem(z + 8 - s, Z)]
        if s:
            up(s - 1).wait_recv()
            mine = mine + RU[s - 1]
        SU[s] = mine
        up(s).start()
        if s < 7:
            mine = tp[lax.rem(z + 9 + s, Z)]
            if s:
                down(s - 1).wait_recv()
                mine = mine + RD[s - 1]
            SD[s] = mine
            down(s).start()
    down(6).wait_recv()
    mine = tp[z] + RD[6]
    up(7).wait_recv()
    PX[0] = mine + RU[7]
    swap = remote(PX.at[0], PX.at[1], px.at[0], px.at[1], core)
    swap.start()
    swap.wait_recv()
    own, other = PX[0], PX[1]
    own = jnp.where(k == 0, own[:, 0:160], own[:, 160:320])
    other = jnp.where(k == 0, other[:, 0:160], other[:, 160:320])
    out[0:40, :] = inv[0:40, :] - jnp.where(k == 0, own, other)
    out[40:80, :] = inv[40:80, :] - jnp.where(k == 0, other, own)
    swap.wait_send()
    for s in range(8):
        up(s).wait_send()
        if s < 7:
            down(s).wait_send()


def shards(anc_inverse, panel, local_rows, inv_diag):
    ids = jnp.pad(local_rows, (0, 16), constant_values=-1)
    live = (ids >= 0).astype(F32)
    rows = jnp.take(anc_inverse, jnp.maximum(ids, 0), axis=0) * live[:, None]
    lst = jnp.broadcast_to(ids.astype(F32)[None, :], (8, 256))
    xt = jnp.pad(panel, ((0, 16), (0, 0))).T.reshape(2, 80, 256)
    vmem = pl.BlockSpec(memory_space=pltpu.VMEM)
    dma = pltpu.SemaphoreType.DMA
    so, tp = pl.pallas_call(
        panel_kernel,
        out_shape=(
            jax.ShapeDtypeStruct((2, 80, 256), F32),
            jax.ShapeDtypeStruct((Z, 40, 384), F32),
        ),
        in_specs=[vmem] * 3,
        out_specs=(vmem, vmem),
        scratch_shapes=[
            pltpu.VMEM((4, 8, 80, 256), F32),
            pltpu.VMEM((2, 8, 256), F32),
            pltpu.VMEM((2, 2, 2, 256, 256), F32),
            pltpu.VMEM((2, 4, 256, 256), BF16),
            pltpu.VMEM((2, 4, 256, 256), BF16),
            pltpu.VMEM((8, 80, 512), F32),
            pltpu.VMEM((8, 80, 512), F32),
            pltpu.VMEM((2, 2, 80, 512), F32),
            pltpu.VMEM((2, 8, 2, 40, 256), F32),
            dma((4, 8 * PARTS)), dma((4, 8 * PARTS)),
            dma((2, PARTS)),
            dma((2, 3)), dma((2,)),
            dma((3,)), dma((3,)),
            dma((8,)), dma((8,)),
            dma((3,)), dma((3,)),
            dma((16,)), dma((2, 8)),
        ],
        compiler_params=pltpu.CompilerParams(collective_id=0, has_side_effects=True),
        name="panel_products",
    )(xt, rows, lst)
    sigma_diag = pl.pallas_call(
        fold_kernel,
        out_shape=jax.ShapeDtypeStruct(inv_diag.shape, F32),
        in_specs=[vmem] * 2,
        out_specs=vmem,
        scratch_shapes=[pltpu.VMEM((8, 40, 384), F32)] * 4
        + [pltpu.VMEM((2, 40, 384), F32)]
        + [dma((8,))] * 4
        + [dma((2,))],
        compiler_params=pltpu.CompilerParams(collective_id=1, has_side_effects=True),
        name="fold_over_rows",
    )(tp, inv_diag)
    sigma_off = so.reshape(160, 256)[:, :240].T
    return (sigma_off, sigma_diag)


def solution(mesh):
    placed = (P("row", "col"), P("row", "col"), P("row"), P("row", "col"))
    return jax.shard_map(
        shards,
        mesh=mesh,
        in_specs=placed,
        out_specs=(P("row", "col"), P("row", "col")),
        check_vma=False,
    )
```

```python
import functools

import jax
import jax.numpy as jnp
from jax import lax
from jax.experimental import pallas as pl
from jax.experimental.pallas import tpu as pltpu
from jax.sharding import PartitionSpec as P

MESH = pl.DeviceIdType.MESH
Z = 16
PARTS = 1
PIECE = 80 // PARTS
HOP = 1
C_RELAY = 4
C_READY = 6
GROUPS = max(8 * PARTS + 3 + 12 * HOP, 10 + C_READY + 7 * PARTS) + 2
FOLDS = ((0, 24), (24, 16))
F32 = jnp.float32
BF16 = jnp.bfloat16


def split(value):
    high = value.astype(BF16)
    return high, (value - high.astype(F32)).astype(BF16)


def dot_nt(a, b):
    return lax.dot_general(a, b, (((1,), (1,)), ((), ())), preferred_element_type=F32)


def dot3(a, b):
    count = a.shape[0] // 2
    both = dot_nt(a, b[0])
    return both[:count] + (both[count:] + dot_nt(a[:count], b[1]))


def stack(value):
    return jnp.concatenate(split(value), axis=0)


def remote(src, dst, send, recv, device):
    return pltpu.make_async_remote_copy(
        src_ref=src, dst_ref=dst, send_sem=send, recv_sem=recv, device_id=device, device_id_type=MESH
    )


def panel_kernel(
    anc, panel, ids, so, diag,
    AV, xt, lst, XR, LB, CB, CH, CL, PB, RB, SG, XZ, tp, FS, FR, PX,
    xs, xr, asend, ls, lr, cs, cr, ds, dr, ss, sr, zs, zr, av, fs, fr, px,
):
    r, c = lax.axis_index("row"), lax.axis_index("col")
    yl, z = lax.div(r, Z), lax.rem(r, Z)
    k, p = lax.rem(c, 2), lax.div(c, 2)
    core = (r, c + 1 - 2 * k)
    across = (lax.rem(r + Z, 2 * Z), c)

    take_anc = pltpu.make_async_copy(anc, AV, av)
    take_anc.start()
    xt[...] = jnp.zeros_like(xt)
    xt[:, :, 0:240] = panel[...].reshape(2, 80, 240)
    lst[...] = jnp.full_like(lst, -1.0)
    lst[:, 0:240] = jnp.broadcast_to(ids[...].astype(F32), (8, 240))

    def at_z(step):
        return (Z * yl + lax.rem(z + step + Z, Z), c)

    up, down = at_z(1), at_z(-1)

    barrier = pltpu.get_barrier_semaphore()
    me = Z * yl + c

    @pl.loop(1, 32)
    def _(o):
        there = lax.rem(me + o, 32)
        pl.semaphore_signal(
            barrier, inc=1, device_id=(Z * lax.div(there, Z) + z, lax.rem(there, Z)), device_id_type=MESH
        )

    for there in (up, down, at_z(5), at_z(-5)):
        pl.semaphore_signal(barrier, inc=1, device_id=there, device_id_type=MESH)
    pl.semaphore_wait(barrier, 35)

    far = jnp.where(yl == lax.div(p, 4), 0, 1)

    def list_place(jj):
        return lax.rem(z - lax.rem(4 * p + 2 * k + jj, Z) + Z, Z)

    def list_slot(jj):
        e = list_place(jj)
        return jnp.minimum(e, Z - e) + far

    for jj in range(2):

        @pl.when((list_place(jj) == 0) & (far == 0))
        def _():
            pltpu.make_async_copy(lst, LB.at[jj], lr.at[jj]).start()

    def list_sends(jj):
        e = list_place(jj)
        return (
            (remote(LB.at[jj], LB.at[jj], ls.at[jj, 0], lr.at[jj], across), (e == 0) & (far == 0)),
            (remote(LB.at[jj], LB.at[jj], ls.at[jj, 1], lr.at[jj], up), e < 8),
            (remote(LB.at[jj], LB.at[jj], ls.at[jj, 2], lr.at[jj], down), (e == 0) | (e > 9)),
        )

    def list_step(jj):
        pltpu.make_async_copy(lst, LB.at[jj], lr.at[jj]).wait()
        for copy, wanted in list_sends(jj):
            pl.when(wanted)(copy.start)

    to_p, to_j = lax.div(r, 4), lax.rem(r, 4)
    turn = 4 * lax.rem(p + to_p, 2) + lax.rem(lax.div(p, 2) - lax.div(to_p, 2) + 4, 4)
    own_n = lax.rem(8 - turn, 8)

    def own_pair(h, part):
        there = XR.at[to_j, own_n, pl.ds(PIECE * part, PIECE)]
        return xt.at[h, pl.ds(PIECE * part, PIECE)], there, xr.at[to_j, PARTS * own_n + part]

    def own_send(h, part):
        src, dst, sem = own_pair(h, part)
        return remote(src, dst, asend.at[h, part], sem, (Z * h + z, 2 * to_p + k))

    def own_local(h):
        return (to_p == p) & (yl == h)

    for jj in range(2):

        @pl.when(list_slot(jj) == 0)
        def _():
            list_step(jj)

    for part in range(PARTS):
        for h in range(2):

            @pl.when(own_local(h))
            def _():
                pltpu.make_async_copy(*own_pair(h, part)).start()

            @pl.when(jnp.logical_not(own_local(h)))
            def _():
                own_send(h, part).start()

    base = lax.rem(4 * p, Z)
    place = jnp.where(k == 0, lax.rem(z - base + Z, Z), lax.rem(base + 3 - z + Z, Z))
    low, late = jnp.minimum(place, 3), jnp.maximum(place - 3, 0)
    onward = at_z(1 - 2 * k)

    def ring(j, n):
        w, part = lax.div(n, PARTS), lax.rem(n, PARTS)
        piece = XR.at[j, w, pl.ds(PIECE * part, PIECE)]
        return remote(piece, piece, xs.at[j, n], xr.at[j, n], onward)

    def behind(i):
        return jnp.where(i <= low, late, 12)

    def line_block(i):
        line = jnp.where(i <= low, low - i, low - i + 4)
        return jnp.where(k == 0, line, 3 - line)

    def forward(g, i):
        n = g - HOP * behind(i) - i

        @pl.when((n >= 0) & (n < 8 * PARTS))
        def _():
            copy = ring(line_block(i), jnp.maximum(n, 0))
            copy.wait_recv()
            pl.when(behind(i) + i < 15)(copy.start)

    tile, tile_half = lax.rem(c, 8), lax.div(c, 8)

    def plane_send(o):
        there = lax.rem(c + o, 16)
        return remote(
            xt.at[:, pl.ds(40 * lax.rem(there, 2), 40)], XZ.at[yl, tile], zs.at[o], zr.at[yl, tile], (Z * tile_half + z, there)
        )

    plane_self = tile_half == yl

    @pl.when(plane_self)
    def _():
        pltpu.make_async_copy(xt.at[:, pl.ds(40 * k, 40)], XZ.at[yl, tile], zr.at[yl, tile]).start()

    def c_core():
        return remote(CB.at[yl, k], CB.at[yl, k], cs.at[0], cr.at[0], core)

    def c_across():
        return remote(CB.at[yl, k], CB.at[yl, k], cs.at[1], cr.at[1], across)

    def c_relay():
        return remote(CB.at[1 - yl, k], CB.at[1 - yl, k], cs.at[2], cr.at[2], core)

    pick_slot = jnp.maximum(list_slot(0), list_slot(1)) + 1
    c_slot = pick_slot + C_READY

    def rows_of(ids):
        hit = lax.broadcasted_iota(jnp.int32, (512, 256), 0).astype(F32) == ids
        return jnp.where(hit, 1.0, 0.0).astype(BF16)

    def pick():
        take_anc.wait()
        own = rows_of(lst[0:1, :])
        hits = [rows_of(LB[jj, 0:1, :]) for jj in range(2)]
        block = AV[...]
        high, mid = split(block)
        rest = ((block - high.astype(F32)) - mid.astype(F32)).astype(BF16)
        found = []
        for part in (high, mid, rest):
            kept = lax.dot_general(own, part, (((0,), (0,)), ((), ())), preferred_element_type=F32).astype(BF16)
            found.append([
                jnp.dot(kept[:, 512 * jj : 512 * jj + 512], hits[jj], preferred_element_type=F32) for jj in range(2)
            ])
        for jj in range(2):
            CB[yl, k, jj] = found[0][jj] + (found[1][jj] + found[2][jj])
        c_across().start()
        c_core().start()

    def c_arrived():
        c_core().wait_recv()
        c_relay().wait_recv()
        for yb in range(2):
            for j in range(4):
                high, low = split(CB[yb, j // 2, j % 2])
                CH[yb, j], CL[yb, j] = high, low

    def peer(w, yb):
        turn = lax.rem(8 - w, 8)
        x, y = lax.rem(lax.div(p, 2) + lax.rem(turn, 4), 4), lax.rem(p + lax.div(turn, 4), 2)
        return remote(PB.at[w, yb], RB.at[w, yb], ds.at[w, yb], dr.at[w, yb], (r, 4 * x + 2 * y + k))

    def multiply(w):
        pieces = [stack(XR[j, w]) for j in range(4)]
        for yb in range(2):
            total = jnp.zeros((80, 256), F32)
            for j in range(4):
                total = total + dot3(pieces[j], (CH[yb, j], CL[yb, j]))
            PB[w, yb] = total

            @pl.when(w > 0)
            def _():
                peer(w, yb).start()

    first_multiply = jnp.maximum(PARTS + 3 + HOP * behind(3), c_slot)

    @pl.loop(0, GROUPS)
    def _(g):
        for jj in range(2):

            @pl.when((g > 0) & (list_slot(jj) == g))
            def _():
                list_step(jj)

        for i in range(4):
            forward(g, i)

        pl.when(g == pick_slot)(pick)

        @pl.when(g == pick_slot + C_RELAY)
        def _():
            c_across().wait_recv()
            c_relay().start()

        @pl.when((g >= 1) & (g <= 16) & jnp.logical_not(plane_self & (g == 1)))
        def _():
            plane_send(g - 1).start()

        pl.when(g == c_slot)(c_arrived)
        ready = g - first_multiply

        @pl.when((ready >= 0) & (ready < 8 * PARTS) & (lax.rem(jnp.maximum(ready, 0), PARTS) == 0))
        def _():
            multiply(lax.div(ready, PARTS))

    def s_copies(yb):
        own, other = SG.at[k, yl, yb], SG.at[k, 1 - yl, yb]
        return (
            remote(own, own, ss.at[0, yb], sr.at[0, yb], across),
            remote(own, own, ss.at[1, yb], sr.at[1, yb], core),
            remote(other, other, ss.at[2, yb], sr.at[2, yb], core),
        )

    for yb in range(2):
        total = PB[0, yb]
        for w in range(1, 8):
            peer(w, yb).wait_recv()
            total = total + RB[w, yb]
        SG[k, yl, yb] = -total
        for copy in s_copies(yb)[:2]:
            copy.start()
    for yb in range(2):
        s_copies(yb)[0].wait_recv()
        s_copies(yb)[2].start()
    so[...] = SG[k, :, yl, :, 0:240]

    for i in range(16):
        pltpu.make_async_copy(xt.at[:, pl.ds(0, 40)], XZ.at[i // 8, i % 8], zr.at[i // 8, i % 8]).wait()
    for yb in range(2):
        for copy in s_copies(yb)[1:]:
            copy.wait_recv()
        side = split(SG[:, :, yb].reshape(320, 256))

        @pl.loop(0, 2)
        def _(half):
            part = pl.ds(8 * half, 8)
            total = dot3(stack(XZ[yb, pl.ds(4 * half, 4)].reshape(320, 256)), side).reshape(8, 40, 320)
            tp[part, :, 0:320] = total + tp[part, :, 0:320] if yb else total

    def fold(way, step, part):
        rows = pl.ds(*FOLDS[part])
        there = at_z(-5 if way else 5) if step == 7 else (down if way else up)
        return remote(
            FS.at[way, step, rows], FR.at[way, step, rows], fs.at[way, step, part], fr.at[way, step, part], there
        )

    def fold_send(way, step, before, distance, part):
        rows = pl.ds(*FOLDS[part])
        mine = tp[lax.rem(z + (Z - distance if way else distance), Z), rows]
        if before is not None:
            fold(way, before, part).wait_recv()
            mine = mine + FR[way, before, rows]
        FS[way, step, rows] = mine
        fold(way, step, part).start()

    for step in range(4):
        for part in range(len(FOLDS)):
            for way in range(2):
                last = 2 + way
                if step < last:
                    fold_send(way, 4 + step, 3 + step if step else None, 7 + way - step, part)
                elif step == last:
                    fold_send(way, 7, 3 + step, 5, part)
        for part in range(len(FOLDS)):
            for way in range(2):
                fold_send(way, step, step - 1 if step else None, 4 - step, part)
    for part in range(len(FOLDS)):
        for way in range(2):
            fold(way, 3, part).wait_recv()
            fold(way, 7, part).wait_recv()
    PX[0] = tp[z] + (FR[0, 3] + FR[1, 3]) + (FR[0, 7] + FR[1, 7])
    swap = remote(PX.at[0], PX.at[1], px.at[0], px.at[1], core)
    swap.start()
    swap.wait_recv()
    own, other = PX[0], PX[1]
    own = jnp.where(k == 0, own[:, 0:160], own[:, 160:320])
    other = jnp.where(k == 0, other[:, 0:160], other[:, 160:320])
    diag[0:40, :] = jnp.where(k == 0, own, other)
    diag[40:80, :] = jnp.where(k == 0, other, own)
    swap.wait_send()
    for step in range(8):
        for part in range(len(FOLDS)):
            fold(1, step, part).wait_send()
            if step != 6:
                fold(0, step, part).wait_send()

    for jj in range(2):
        for copy, wanted in list_sends(jj):
            pl.when(wanted)(copy.wait_send)
    for h in range(2):
        for part in range(PARTS):
            pl.when(jnp.logical_not(own_local(h)))(own_send(h, part).wait_send)

    @pl.loop(0, 16)
    def _(n):
        pl.when(jnp.logical_not(plane_self & (n == 0)))(plane_send(n).wait_send)

    for i in range(4):

        @pl.when(behind(i) + i < 15)
        def _():
            @pl.loop(0, 8 * PARTS)
            def _(n):
                ring(line_block(i), n).wait_send()

    for copy in (c_core(), c_across(), c_relay(), *s_copies(0), *s_copies(1)):
        copy.wait_send()

    @pl.loop(1, 8)
    def _(w):
        peer(w, 0).wait_send()
        peer(w, 1).wait_send()


def shards(anc_inverse, panel, local_rows, inv_diag):
    vmem = pl.BlockSpec(memory_space=pltpu.VMEM)
    dma = pltpu.SemaphoreType.DMA
    so, folded = pl.pallas_call(
        panel_kernel,
        out_shape=(
            jax.ShapeDtypeStruct((2, 80, 240), F32),
            jax.ShapeDtypeStruct(inv_diag.shape, F32),
        ),
        in_specs=[pl.BlockSpec(memory_space=pl.ANY), vmem, vmem],
        out_specs=(vmem, vmem),
        scratch_shapes=[
            pltpu.VMEM((512, 1024), F32),
            pltpu.VMEM((2, 80, 256), F32),
            pltpu.VMEM((8, 256), F32),
            pltpu.VMEM((4, 8, 80, 256), F32),
            pltpu.VMEM((2, 8, 256), F32),
            pltpu.VMEM((2, 2, 2, 256, 256), F32),
            pltpu.VMEM((2, 4, 256, 256), BF16),
            pltpu.VMEM((2, 4, 256, 256), BF16),
            pltpu.VMEM((8, 2, 80, 256), F32),
            pltpu.VMEM((8, 2, 80, 256), F32),
            pltpu.VMEM((2, 2, 2, 80, 256), F32),
            pltpu.VMEM((2, 8, 2, 40, 256), F32),
            pltpu.VMEM((Z, 40, 384), F32),
            pltpu.VMEM((2, 8, 40, 384), F32),
            pltpu.VMEM((2, 8, 40, 384), F32),
            pltpu.VMEM((2, 40, 384), F32),
            dma((4, 8 * PARTS)), dma((4, 8 * PARTS)),
            dma((2, PARTS)),
            dma((2, 3)), dma((2,)),
            dma((3,)), dma((3,)),
            dma((8, 2)), dma((8, 2)),
            dma((3, 2)), dma((3, 2)),
            dma((16,)), dma((2, 8)),
            dma, dma((2, 8, 2)), dma((2, 8, 2)), dma((2,)),
        ],
        compiler_params=pltpu.CompilerParams(collective_id=0, has_side_effects=True),
        name="panel_products",
    )(anc_inverse, panel.T, local_rows.reshape(1, -1))
    sigma_diag = inv_diag - folded
    sigma_off = so.reshape(160, 240).T
    return (sigma_off, sigma_diag)


def solution(mesh):
    placed = (P("row", "col"), P("row", "col"), P("row"), P("row", "col"))
    return jax.shard_map(
        shards,
        mesh=mesh,
        in_specs=placed,
        out_specs=(P("row", "col"), P("row", "col")),
        check_vma=False,
    )
```

```python
import functools

import jax
import jax.numpy as jnp
from jax import lax
from jax.experimental import pallas as pl
from jax.experimental.pallas import tpu as pltpu
from jax.sharding import PartitionSpec as P

MESH = pl.DeviceIdType.MESH
Z = 16
HOP = 1
C_RELAY = 4
C_READY = 6
GROUPS = max(9 + 3 + 12 * HOP, 10 + C_READY + 9) + 2
FOLDS = ((0, 24), (24, 16))
F32 = jnp.float32
BF16 = jnp.bfloat16


def split(value):
    high = value.astype(BF16)
    return high, (value - high.astype(F32)).astype(BF16)


def dot_nt(a, b):
    return lax.dot_general(a, b, (((1,), (1,)), ((), ())), preferred_element_type=F32)


def dot3(a, b):
    count = a.shape[0] // 2
    both = dot_nt(a, b[0])
    return both[:count] + (both[count:] + dot_nt(a[:count], b[1]))


def stack(value):
    return jnp.concatenate(split(value), axis=0)


def remote(src, dst, send, recv, device):
    return pltpu.make_async_remote_copy(
        src_ref=src, dst_ref=dst, send_sem=send, recv_sem=recv, device_id=device, device_id_type=MESH
    )


def panel_kernel(
    anc, panel, ids, so, diag,
    AV, xt, lst, XR, LB, CB, CH, CL, PB, RB, SG, XZ, tp, FS, FR, PX,
    xs, hs, xr, asend, ls, lr, cs, cr, ds, dr, ss, sr, zs, zr, av, fs, fr, px,
):
    r, c = lax.axis_index("row"), lax.axis_index("col")
    yl, z = lax.div(r, Z), lax.rem(r, Z)
    k, p = lax.rem(c, 2), lax.div(c, 2)
    core = (r, c + 1 - 2 * k)
    across = (lax.rem(r + Z, 2 * Z), c)

    take_anc = pltpu.make_async_copy(anc, AV, av)
    take_anc.start()
    xt[...] = jnp.zeros_like(xt)
    xt[:, :, 0:240] = panel[...].reshape(2, 80, 240)
    lst[...] = jnp.full_like(lst, -1.0)
    lst[:, 0:240] = jnp.broadcast_to(ids[...].astype(F32), (8, 240))

    def at_z(step):
        return (Z * yl + lax.rem(z + step + Z, Z), c)

    up, down = at_z(1), at_z(-1)

    barrier = pltpu.get_barrier_semaphore()
    me = Z * yl + c

    @pl.loop(1, 32)
    def _(o):
        there = lax.rem(me + o, 32)
        pl.semaphore_signal(
            barrier, inc=1, device_id=(Z * lax.div(there, Z) + z, lax.rem(there, Z)), device_id_type=MESH
        )

    for there in (up, down, at_z(5), at_z(-5)):
        pl.semaphore_signal(barrier, inc=1, device_id=there, device_id_type=MESH)
    pl.semaphore_wait(barrier, 35)

    far = jnp.where(yl == lax.div(p, 4), 0, 1)

    def list_place(jj):
        return lax.rem(z - lax.rem(4 * p + 2 * k + jj, Z) + Z, Z)

    def list_slot(jj):
        e = list_place(jj)
        return jnp.minimum(e, Z - e) + far

    for jj in range(2):

        @pl.when((list_place(jj) == 0) & (far == 0))
        def _():
            pltpu.make_async_copy(lst, LB.at[jj], lr.at[jj]).start()

    def list_sends(jj):
        e = list_place(jj)
        return (
            (remote(LB.at[jj], LB.at[jj], ls.at[jj, 0], lr.at[jj], across), (e == 0) & (far == 0)),
            (remote(LB.at[jj], LB.at[jj], ls.at[jj, 1], lr.at[jj], up), e < 8),
            (remote(LB.at[jj], LB.at[jj], ls.at[jj, 2], lr.at[jj], down), (e == 0) | (e > 9)),
        )

    def list_step(jj):
        pltpu.make_async_copy(lst, LB.at[jj], lr.at[jj]).wait()
        for copy, wanted in list_sends(jj):
            pl.when(wanted)(copy.start)

    to_p, to_j = lax.div(r, 4), lax.rem(r, 4)
    turn = 4 * lax.rem(p + to_p, 2) + lax.rem(lax.div(p, 2) - lax.div(to_p, 2) + 4, 4)
    own_n = lax.rem(8 - turn, 8)

    lent = (k == 0) & (own_n == 7)
    own_at = jnp.where(k == 1, own_n + jnp.minimum(own_n, 1), jnp.where(lent, 1, own_n))

    def own_pair(h):
        return xt.at[h], XR.at[to_j, own_at], xr.at[to_j, own_at]

    def own_send(h):
        src, dst, sem = own_pair(h)
        return remote(src, dst, asend.at[h], sem, (Z * h + z, 2 * to_p + jnp.where(lent, 1, k)))

    def own_local(h):
        return (to_p == p) & (yl == h)

    for jj in range(2):

        @pl.when(list_slot(jj) == 0)
        def _():
            list_step(jj)

    for h in range(2):

        @pl.when(own_local(h))
        def _():
            pltpu.make_async_copy(*own_pair(h)).start()

        @pl.when(jnp.logical_not(own_local(h)))
        def _():
            own_send(h).start()

    base = lax.rem(4 * p, Z)
    place = jnp.where(k == 0, lax.rem(z - base + Z, Z), lax.rem(base + 3 - z + Z, Z))
    low, late = jnp.minimum(place, 3), jnp.maximum(place - 3, 0)
    onward = at_z(1 - 2 * k)

    pieces_here = 7 + 2 * k

    def ring(j, n):
        return remote(XR.at[j, n], XR.at[j, n], xs.at[j, n], xr.at[j, n], onward)

    def hand_over(j):
        return remote(XR.at[j, 1], XR.at[j, 7], hs.at[j], xr.at[j, 7], core)

    def behind(i):
        return jnp.where(i <= low, late, 12)

    def line_block(i):
        line = jnp.where(i <= low, low - i, low - i + 4)
        return jnp.where(k == 0, line, 3 - line)

    def forward(g, i):
        n = g - HOP * behind(i) - i

        @pl.when((n >= 0) & (n < pieces_here))
        def _():
            j = line_block(i)
            copy = ring(j, jnp.maximum(n, 0))
            copy.wait_recv()
            pl.when(behind(i) + i < 15)(copy.start)
            pl.when((k == 1) & (n == 1))(hand_over(j).start)

    tile, tile_half = lax.rem(c, 8), lax.div(c, 8)

    def plane_send(o):
        there = lax.rem(c + o, 16)
        return remote(
            xt.at[:, pl.ds(40 * lax.rem(there, 2), 40)], XZ.at[yl, tile], zs.at[o], zr.at[yl, tile], (Z * tile_half + z, there)
        )

    plane_self = tile_half == yl

    @pl.when(plane_self)
    def _():
        pltpu.make_async_copy(xt.at[:, pl.ds(40 * k, 40)], XZ.at[yl, tile], zr.at[yl, tile]).start()

    def c_core():
        return remote(CB.at[yl, k], CB.at[yl, k], cs.at[0], cr.at[0], core)

    def c_across():
        return remote(CB.at[yl, k], CB.at[yl, k], cs.at[1], cr.at[1], across)

    def c_relay():
        return remote(CB.at[1 - yl, k], CB.at[1 - yl, k], cs.at[2], cr.at[2], core)

    pick_slot = jnp.maximum(list_slot(0), list_slot(1)) + 1
    c_slot = pick_slot + C_READY

    def rows_of(ids):
        hit = lax.broadcasted_iota(jnp.int32, (512, 256), 0).astype(F32) == ids
        return jnp.where(hit, 1.0, 0.0).astype(BF16)

    def pick():
        take_anc.wait()
        own = rows_of(lst[0:1, :])
        hits = [rows_of(LB[jj, 0:1, :]) for jj in range(2)]
        block = AV[...]
        high, mid = split(block)
        rest = ((block - high.astype(F32)) - mid.astype(F32)).astype(BF16)
        found = []
        for part in (high, mid, rest):
            kept = lax.dot_general(own, part, (((0,), (0,)), ((), ())), preferred_element_type=F32).astype(BF16)
            found.append([
                jnp.dot(kept[:, 512 * jj : 512 * jj + 512], hits[jj], preferred_element_type=F32) for jj in range(2)
            ])
        for jj in range(2):
            CB[yl, k, jj] = found[0][jj] + (found[1][jj] + found[2][jj])
        c_across().start()
        c_core().start()

    def c_arrived():
        c_core().wait_recv()
        c_relay().wait_recv()
        for yb in range(2):
            for j in range(4):
                high, low = split(CB[yb, j // 2, j % 2])
                CH[yb, j], CL[yb, j] = high, low

    def peer(w, yb):
        turn = lax.rem(8 - w, 8)
        x, y = lax.rem(lax.div(p, 2) + lax.rem(turn, 4), 4), lax.rem(p + lax.div(turn, 4), 2)
        return remote(PB.at[w, yb], RB.at[w, yb], ds.at[w, yb], dr.at[w, yb], (r, 4 * x + 2 * y + k))

    def multiply(w):
        at = jnp.where(k == 1, w + jnp.minimum(w, 1), w)
        pieces = [stack(XR[j, at]) for j in range(4)]
        for yb in range(2):
            total = jnp.zeros((80, 256), F32)
            for j in range(4):
                total = total + dot3(pieces[j], (CH[yb, j], CL[yb, j]))
            PB[w, yb] = total

            @pl.when(w > 0)
            def _():
                peer(w, yb).start()

    first_multiply = jnp.maximum(1 + 3 + HOP * behind(3), c_slot)

    @pl.loop(0, GROUPS)
    def _(g):
        for jj in range(2):

            @pl.when((g > 0) & (list_slot(jj) == g))
            def _():
                list_step(jj)

        for i in range(4):
            forward(g, i)

        pl.when(g == pick_slot)(pick)

        @pl.when(g == pick_slot + C_RELAY)
        def _():
            c_across().wait_recv()
            c_relay().start()

        @pl.when((g >= 1) & (g <= 16) & jnp.logical_not(plane_self & (g == 1)))
        def _():
            plane_send(g - 1).start()

        pl.when(g == c_slot)(c_arrived)
        ready = g - first_multiply

        @pl.when((ready >= 0) & (ready < pieces_here) & ((k == 0) | (ready != 1)))
        def _():
            multiply(jnp.maximum(ready - jnp.where(ready > 1, k, 0), 0))

    @pl.when(k == 0)
    def _():
        for j in range(4):
            ring(j, 7).wait_recv()
        multiply(7)

    def s_copies(yb):
        own, other = SG.at[k, yl, yb], SG.at[k, 1 - yl, yb]
        return (
            remote(own, own, ss.at[0, yb], sr.at[0, yb], across),
            remote(own, own, ss.at[1, yb], sr.at[1, yb], core),
            remote(other, other, ss.at[2, yb], sr.at[2, yb], core),
        )

    for yb in range(2):
        total = PB[0, yb]
        for w in range(1, 8):
            peer(w, yb).wait_recv()
            total = total + RB[w, yb]
        SG[k, yl, yb] = -total
        for copy in s_copies(yb)[:2]:
            copy.start()
    for yb in range(2):
        s_copies(yb)[0].wait_recv()
        s_copies(yb)[2].start()
    so[...] = SG[k, :, yl, :, 0:240]

    for i in range(16):
        pltpu.make_async_copy(xt.at[:, pl.ds(0, 40)], XZ.at[i // 8, i % 8], zr.at[i // 8, i % 8]).wait()
    for yb in range(2):
        for copy in s_copies(yb)[1:]:
            copy.wait_recv()
        side = split(SG[:, :, yb].reshape(320, 256))

        @pl.loop(0, 2)
        def _(half):
            part = pl.ds(8 * half, 8)
            total = dot3(stack(XZ[yb, pl.ds(4 * half, 4)].reshape(320, 256)), side).reshape(8, 40, 320)
            tp[part, :, 0:320] = total + tp[part, :, 0:320] if yb else total

    def fold(way, step, part):
        rows = pl.ds(*FOLDS[part])
        there = at_z(-5 if way else 5) if step == 7 else (down if way else up)
        return remote(
            FS.at[way, step, rows], FR.at[way, step, rows], fs.at[way, step, part], fr.at[way, step, part], there
        )

    def fold_send(way, step, before, distance, part):
        rows = pl.ds(*FOLDS[part])
        mine = tp[lax.rem(z + (Z - distance if way else distance), Z), rows]
        if before is not None:
            fold(way, before, part).wait_recv()
            mine = mine + FR[way, before, rows]
        FS[way, step, rows] = mine
        fold(way, step, part).start()

    for step in range(4):
        for part in range(len(FOLDS)):
            for way in range(2):
                last = 2 + way
                if step < last:
                    fold_send(way, 4 + step, 3 + step if step else None, 7 + way - step, part)
                elif step == last:
                    fold_send(way, 7, 3 + step, 5, part)
        for part in range(len(FOLDS)):
            for way in range(2):
                fold_send(way, step, step - 1 if step else None, 4 - step, part)
    for part in range(len(FOLDS)):
        for way in range(2):
            fold(way, 3, part).wait_recv()
            fold(way, 7, part).wait_recv()
    PX[0] = tp[z] + (FR[0, 3] + FR[1, 3]) + (FR[0, 7] + FR[1, 7])
    swap = remote(PX.at[0], PX.at[1], px.at[0], px.at[1], core)
    swap.start()
    swap.wait_recv()
    own, other = PX[0], PX[1]
    own = jnp.where(k == 0, own[:, 0:160], own[:, 160:320])
    other = jnp.where(k == 0, other[:, 0:160], other[:, 160:320])
    diag[0:40, :] = jnp.where(k == 0, own, other)
    diag[40:80, :] = jnp.where(k == 0, other, own)
    swap.wait_send()
    for step in range(8):
        for part in range(len(FOLDS)):
            fold(1, step, part).wait_send()
            if step != 6:
                fold(0, step, part).wait_send()

    for jj in range(2):
        for copy, wanted in list_sends(jj):
            pl.when(wanted)(copy.wait_send)
    for h in range(2):
        pl.when(jnp.logical_not(own_local(h)))(own_send(h).wait_send)

    @pl.loop(0, 16)
    def _(n):
        pl.when(jnp.logical_not(plane_self & (n == 0)))(plane_send(n).wait_send)

    for i in range(4):

        @pl.when(behind(i) + i < 15)
        def _():
            @pl.loop(0, pieces_here)
            def _(n):
                ring(line_block(i), n).wait_send()

    for j in range(4):
        pl.when(k == 1)(hand_over(j).wait_send)

    for copy in (c_core(), c_across(), c_relay(), *s_copies(0), *s_copies(1)):
        copy.wait_send()

    @pl.loop(1, 8)
    def _(w):
        peer(w, 0).wait_send()
        peer(w, 1).wait_send()


def shards(anc_inverse, panel, local_rows, inv_diag):
    vmem = pl.BlockSpec(memory_space=pltpu.VMEM)
    dma = pltpu.SemaphoreType.DMA
    so, folded = pl.pallas_call(
        panel_kernel,
        out_shape=(
            jax.ShapeDtypeStruct((2, 80, 240), F32),
            jax.ShapeDtypeStruct(inv_diag.shape, F32),
        ),
        in_specs=[pl.BlockSpec(memory_space=pl.ANY), vmem, vmem],
        out_specs=(vmem, vmem),
        scratch_shapes=[
            pltpu.VMEM((512, 1024), F32),
            pltpu.VMEM((2, 80, 256), F32),
            pltpu.VMEM((8, 256), F32),
            pltpu.VMEM((4, 9, 80, 256), F32),
            pltpu.VMEM((2, 8, 256), F32),
            pltpu.VMEM((2, 2, 2, 256, 256), F32),
            pltpu.VMEM((2, 4, 256, 256), BF16),
            pltpu.VMEM((2, 4, 256, 256), BF16),
            pltpu.VMEM((8, 2, 80, 256), F32),
            pltpu.VMEM((8, 2, 80, 256), F32),
            pltpu.VMEM((2, 2, 2, 80, 256), F32),
            pltpu.VMEM((2, 8, 2, 40, 256), F32),
            pltpu.VMEM((Z, 40, 384), F32),
            pltpu.VMEM((2, 8, 40, 384), F32),
            pltpu.VMEM((2, 8, 40, 384), F32),
            pltpu.VMEM((2, 40, 384), F32),
            dma((4, 9)), dma((4,)), dma((4, 9)),
            dma((2,)),
            dma((2, 3)), dma((2,)),
            dma((3,)), dma((3,)),
            dma((8, 2)), dma((8, 2)),
            dma((3, 2)), dma((3, 2)),
            dma((16,)), dma((2, 8)),
            dma, dma((2, 8, 2)), dma((2, 8, 2)), dma((2,)),
        ],
        compiler_params=pltpu.CompilerParams(collective_id=0, has_side_effects=True),
        name="panel_products",
    )(anc_inverse, panel.T, local_rows.reshape(1, -1))
    sigma_diag = inv_diag - folded
    sigma_off = so.reshape(160, 240).T
    return (sigma_off, sigma_diag)


def solution(mesh):
    placed = (P("row", "col"), P("row", "col"), P("row"), P("row", "col"))
    return jax.shard_map(
        shards,
        mesh=mesh,
        in_specs=placed,
        out_specs=(P("row", "col"), P("row", "col")),
        check_vma=False,
    )
```

```python
import functools

import jax
import jax.numpy as jnp
from jax import lax
from jax.experimental import pallas as pl
from jax.experimental.pallas import tpu as pltpu
from jax.sharding import PartitionSpec as P

MESH = pl.DeviceIdType.MESH
Z = 16
HOP = 1
C_RELAY = 4
C_READY = 6
GROUPS = max(9 + 3 + 12 * HOP, 10 + C_READY + 9) + 2
FOLDS = ((0, 24), (24, 16))
F32 = jnp.float32
BF16 = jnp.bfloat16


def split(value):
    high = value.astype(BF16)
    return high, (value - high.astype(F32)).astype(BF16)


def dot_nt(a, b):
    return lax.dot_general(a, b, (((1,), (1,)), ((), ())), preferred_element_type=F32)


def dot3(a, b):
    count = a.shape[0] // 2
    both = dot_nt(a, b[0])
    return both[:count] + (both[count:] + dot_nt(a[:count], b[1]))


def stack(value):
    return jnp.concatenate(split(value), axis=0)


def remote(src, dst, send, recv, device):
    return pltpu.make_async_remote_copy(
        src_ref=src, dst_ref=dst, send_sem=send, recv_sem=recv, device_id=device, device_id_type=MESH
    )


def panel_kernel(
    anc, panel, ids, so, diag,
    AV, xt, lst, XR, LB, CB, CH, CL, PB, RB, SG, XZ, tp, FS, FR, PX,
    xs, hs, xr, asend, ls, lr, cs, cr, ds, dr, ss, sr, zs, zr, av, fs, fr, px,
):
    r, c = lax.axis_index("row"), lax.axis_index("col")
    yl, z = lax.div(r, Z), lax.rem(r, Z)
    k, p = lax.rem(c, 2), lax.div(c, 2)
    core = (r, c + 1 - 2 * k)
    across = (lax.rem(r + Z, 2 * Z), c)

    take_anc = pltpu.make_async_copy(anc, AV, av)
    take_anc.start()
    xt[...] = jnp.zeros_like(xt)
    xt[:, :, 0:240] = panel[...].reshape(2, 80, 240)
    lst[...] = jnp.full_like(lst, -1.0)
    lst[:, 0:240] = jnp.broadcast_to(ids[...].astype(F32), (8, 240))

    def at_z(step):
        return (Z * yl + lax.rem(z + step + Z, Z), c)

    up, down = at_z(1), at_z(-1)

    barrier = pltpu.get_barrier_semaphore()
    me = Z * yl + c

    @pl.loop(1, 32)
    def _(o):
        there = lax.rem(me + o, 32)
        pl.semaphore_signal(
            barrier, inc=1, device_id=(Z * lax.div(there, Z) + z, lax.rem(there, Z)), device_id_type=MESH
        )

    for there in (up, down, at_z(5), at_z(-5)):
        pl.semaphore_signal(barrier, inc=1, device_id=there, device_id_type=MESH)
    pl.semaphore_wait(barrier, 35)

    far = jnp.where(yl == lax.div(p, 4), 0, 1)

    def list_place(jj):
        return lax.rem(z - lax.rem(4 * p + 2 * k + jj, Z) + Z, Z)

    def list_slot(jj):
        e = list_place(jj)
        return jnp.minimum(e, Z - e) + far

    for jj in range(2):

        @pl.when((list_place(jj) == 0) & (far == 0))
        def _():
            pltpu.make_async_copy(lst, LB.at[jj], lr.at[jj]).start()

    def list_sends(jj):
        e = list_place(jj)
        return (
            (remote(LB.at[jj], LB.at[jj], ls.at[jj, 0], lr.at[jj], across), (e == 0) & (far == 0)),
            (remote(LB.at[jj], LB.at[jj], ls.at[jj, 1], lr.at[jj], up), e < 8),
            (remote(LB.at[jj], LB.at[jj], ls.at[jj, 2], lr.at[jj], down), (e == 0) | (e > 9)),
        )

    def list_step(jj):
        pltpu.make_async_copy(lst, LB.at[jj], lr.at[jj]).wait()
        for copy, wanted in list_sends(jj):
            pl.when(wanted)(copy.start)

    to_p, to_j = lax.div(r, 4), lax.rem(r, 4)
    turn = 4 * lax.rem(p + to_p, 2) + lax.rem(lax.div(p, 2) - lax.div(to_p, 2) + 4, 4)
    own_n = lax.rem(8 - turn, 8)

    lent = (k == 0) & (own_n == 7)
    own_at = jnp.where(k == 1, own_n + jnp.minimum(own_n, 1), jnp.where(lent, 1, own_n))

    def own_pair(h):
        return xt.at[h], XR.at[to_j, own_at], xr.at[to_j, own_at]

    def own_send(h):
        src, dst, sem = own_pair(h)
        return remote(src, dst, asend.at[h], sem, (Z * h + z, 2 * to_p + jnp.where(lent, 1, k)))

    def own_local(h):
        return (to_p == p) & (yl == h)

    for jj in range(2):

        @pl.when(list_slot(jj) == 0)
        def _():
            list_step(jj)

    for h in range(2):

        @pl.when(own_local(h))
        def _():
            pltpu.make_async_copy(*own_pair(h)).start()

        @pl.when(jnp.logical_not(own_local(h)))
        def _():
            own_send(h).start()

    base = lax.rem(4 * p, Z)
    place = jnp.where(k == 0, lax.rem(z - base + Z, Z), lax.rem(base + 3 - z + Z, Z))
    low, late = jnp.minimum(place, 3), jnp.maximum(place - 3, 0)
    onward = at_z(1 - 2 * k)

    pieces_here = 7 + 2 * k

    def ring(j, n):
        return remote(XR.at[j, n], XR.at[j, n], xs.at[j, n], xr.at[j, n], onward)

    def hand_over(j):
        return remote(XR.at[j, 1], XR.at[j, 7], hs.at[j], xr.at[j, 7], core)

    def behind(i):
        return jnp.where(i <= low, late, 12)

    def line_block(i):
        line = jnp.where(i <= low, low - i, low - i + 4)
        return jnp.where(k == 0, line, 3 - line)

    def forward(g, i):
        n = g - HOP * behind(i) - i

        @pl.when((n >= 0) & (n < pieces_here))
        def _():
            j = line_block(i)
            copy = ring(j, jnp.maximum(n, 0))
            copy.wait_recv()
            pl.when(behind(i) + i < 15)(copy.start)
            pl.when((k == 1) & (n == 1))(hand_over(j).start)

    tile, tile_half = lax.rem(c, 8), lax.div(c, 8)

    def plane_send(o):
        there = lax.rem(c + o, 16)
        return remote(
            xt.at[:, pl.ds(40 * lax.rem(there, 2), 40)], XZ.at[yl, tile], zs.at[o], zr.at[yl, tile], (Z * tile_half + z, there)
        )

    plane_self = tile_half == yl

    @pl.when(plane_self)
    def _():
        pltpu.make_async_copy(xt.at[:, pl.ds(40 * k, 40)], XZ.at[yl, tile], zr.at[yl, tile]).start()

    def c_core():
        return remote(CB.at[yl, k], CB.at[yl, k], cs.at[0], cr.at[0], core)

    def c_across():
        return remote(CB.at[yl, k], CB.at[yl, k], cs.at[1], cr.at[1], across)

    def c_relay():
        return remote(CB.at[1 - yl, k], CB.at[1 - yl, k], cs.at[2], cr.at[2], core)

    pick_slot = jnp.maximum(list_slot(0), list_slot(1)) + 1
    c_slot = pick_slot + C_READY

    def rows_of(ids):
        hit = lax.broadcasted_iota(jnp.int32, (512, 256), 0).astype(F32) == ids
        return jnp.where(hit, 1.0, 0.0).astype(BF16)

    def pick():
        take_anc.wait()
        own = rows_of(lst[0:1, :])
        hits = [rows_of(LB[jj, 0:1, :]) for jj in range(2)]
        block = AV[...]
        high, mid = split(block)
        rest = ((block - high.astype(F32)) - mid.astype(F32)).astype(BF16)
        found = []
        for part in (high, mid, rest):
            kept = lax.dot_general(own, part, (((0,), (0,)), ((), ())), preferred_element_type=F32).astype(BF16)
            found.append([
                jnp.dot(kept[:, 512 * jj : 512 * jj + 512], hits[jj], preferred_element_type=F32) for jj in range(2)
            ])
        for jj in range(2):
            CB[yl, k, jj] = found[0][jj] + (found[1][jj] + found[2][jj])
        c_across().start()
        c_core().start()

    def c_arrived():
        c_core().wait_recv()
        c_relay().wait_recv()
        for yb in range(2):
            for j in range(4):
                high, low = split(CB[yb, j // 2, j % 2])
                CH[yb, j], CL[yb, j] = high, low

    def peer(w, yb):
        turn = lax.rem(8 - w, 8)
        x, y = lax.rem(lax.div(p, 2) + lax.rem(turn, 4), 4), lax.rem(p + lax.div(turn, 4), 2)
        return remote(PB.at[w, yb], RB.at[w, yb], ds.at[w, yb], dr.at[w, yb], (r, 4 * x + 2 * y + k))

    def multiply(w):
        at = jnp.where(k == 1, w + jnp.minimum(w, 1), w)
        pieces = [stack(XR[j, at]) for j in range(4)]
        for yb in range(2):
            total = jnp.zeros((80, 256), F32)
            for j in range(4):
                total = total + dot3(pieces[j], (CH[yb, j], CL[yb, j]))
            PB[w, yb] = total

            @pl.when(w > 0)
            def _():
                peer(w, yb).start()

    first_multiply = jnp.maximum(1 + 3 + HOP * behind(3), c_slot)

    @pl.loop(0, GROUPS)
    def _(g):
        for jj in range(2):

            @pl.when((g > 0) & (list_slot(jj) == g))
            def _():
                list_step(jj)

        for i in range(4):
            forward(g, i)

        pl.when(g == pick_slot)(pick)

        @pl.when(g == pick_slot + C_RELAY)
        def _():
            c_across().wait_recv()
            c_relay().start()

        due = g - HOP * late - 1

        @pl.when((due >= 0) & (due < 8))
        def _():
            pl.when(jnp.logical_not(plane_self & (due == 0)))(plane_send(2 * due).start)
            plane_send(2 * due + 1).start()

        pl.when(g == c_slot)(c_arrived)
        ready = g - first_multiply

        @pl.when((ready >= 0) & (ready < pieces_here) & ((k == 0) | (ready != 1)))
        def _():
            multiply(jnp.maximum(ready - jnp.where(ready > 1, k, 0), 0))

    @pl.when(k == 0)
    def _():
        for j in range(4):
            ring(j, 7).wait_recv()
        multiply(7)

    def s_copies(yb):
        own, other = SG.at[k, yl, yb], SG.at[k, 1 - yl, yb]
        return (
            remote(own, own, ss.at[0, yb], sr.at[0, yb], across),
            remote(own, own, ss.at[1, yb], sr.at[1, yb], core),
            remote(other, other, ss.at[2, yb], sr.at[2, yb], core),
        )

    for yb in range(2):
        total = PB[0, yb]
        for w in range(1, 8):
            peer(w, yb).wait_recv()
            total = total + RB[w, yb]
        SG[k, yl, yb] = -total
        for copy in s_copies(yb)[:2]:
            copy.start()
    for yb in range(2):
        s_copies(yb)[0].wait_recv()
        s_copies(yb)[2].start()
    so[...] = SG[k, :, yl, :, 0:240]

    for i in range(16):
        pltpu.make_async_copy(xt.at[:, pl.ds(0, 40)], XZ.at[i // 8, i % 8], zr.at[i // 8, i % 8]).wait()
    for yb in range(2):
        for copy in s_copies(yb)[1:]:
            copy.wait_recv()
        side = split(SG[:, :, yb].reshape(320, 256))

        @pl.loop(0, 2)
        def _(half):
            part = pl.ds(8 * half, 8)
            total = dot3(stack(XZ[yb, pl.ds(4 * half, 4)].reshape(320, 256)), side).reshape(8, 40, 320)
            tp[part, :, 0:320] = total + tp[part, :, 0:320] if yb else total

    def fold(way, step, part):
        rows = pl.ds(*FOLDS[part])
        there = at_z(-5 if way else 5) if step == 7 else (down if way else up)
        return remote(
            FS.at[way, step, rows], FR.at[way, step, rows], fs.at[way, step, part], fr.at[way, step, part], there
        )

    def fold_send(way, step, before, distance, part):
        rows = pl.ds(*FOLDS[part])
        mine = tp[lax.rem(z + (Z - distance if way else distance), Z), rows]
        if before is not None:
            fold(way, before, part).wait_recv()
            mine = mine + FR[way, before, rows]
        FS[way, step, rows] = mine
        fold(way, step, part).start()

    for step in range(4):
        for part in range(len(FOLDS)):
            for way in range(2):
                last = 2 + way
                if step < last:
                    fold_send(way, 4 + step, 3 + step if step else None, 7 + way - step, part)
                elif step == last:
                    fold_send(way, 7, 3 + step, 5, part)
        for part in range(len(FOLDS)):
            for way in range(2):
                fold_send(way, step, step - 1 if step else None, 4 - step, part)
    for part in range(len(FOLDS)):
        for way in range(2):
            fold(way, 3, part).wait_recv()
            fold(way, 7, part).wait_recv()
    PX[0] = tp[z] + (FR[0, 3] + FR[1, 3]) + (FR[0, 7] + FR[1, 7])
    swap = remote(PX.at[0], PX.at[1], px.at[0], px.at[1], core)
    swap.start()
    swap.wait_recv()
    own, other = PX[0], PX[1]
    own = jnp.where(k == 0, own[:, 0:160], own[:, 160:320])
    other = jnp.where(k == 0, other[:, 0:160], other[:, 160:320])
    diag[0:40, :] = jnp.where(k == 0, own, other)
    diag[40:80, :] = jnp.where(k == 0, other, own)
    swap.wait_send()
    for step in range(8):
        for part in range(len(FOLDS)):
            fold(1, step, part).wait_send()
            if step != 6:
                fold(0, step, part).wait_send()

    for jj in range(2):
        for copy, wanted in list_sends(jj):
            pl.when(wanted)(copy.wait_send)
    for h in range(2):
        pl.when(jnp.logical_not(own_local(h)))(own_send(h).wait_send)

    @pl.loop(0, 16)
    def _(n):
        pl.when(jnp.logical_not(plane_self & (n == 0)))(plane_send(n).wait_send)

    for i in range(4):

        @pl.when(behind(i) + i < 15)
        def _():
            @pl.loop(0, pieces_here)
            def _(n):
                ring(line_block(i), n).wait_send()

    for j in range(4):
        pl.when(k == 1)(hand_over(j).wait_send)

    for copy in (c_core(), c_across(), c_relay(), *s_copies(0), *s_copies(1)):
        copy.wait_send()

    @pl.loop(1, 8)
    def _(w):
        peer(w, 0).wait_send()
        peer(w, 1).wait_send()


def shards(anc_inverse, panel, local_rows, inv_diag):
    vmem = pl.BlockSpec(memory_space=pltpu.VMEM)
    dma = pltpu.SemaphoreType.DMA
    so, folded = pl.pallas_call(
        panel_kernel,
        out_shape=(
            jax.ShapeDtypeStruct((2, 80, 240), F32),
            jax.ShapeDtypeStruct(inv_diag.shape, F32),
        ),
        in_specs=[pl.BlockSpec(memory_space=pl.ANY), vmem, vmem],
        out_specs=(vmem, vmem),
        scratch_shapes=[
            pltpu.VMEM((512, 1024), F32),
            pltpu.VMEM((2, 80, 256), F32),
            pltpu.VMEM((8, 256), F32),
            pltpu.VMEM((4, 9, 80, 256), F32),
            pltpu.VMEM((2, 8, 256), F32),
            pltpu.VMEM((2, 2, 2, 256, 256), F32),
            pltpu.VMEM((2, 4, 256, 256), BF16),
            pltpu.VMEM((2, 4, 256, 256), BF16),
            pltpu.VMEM((8, 2, 80, 256), F32),
            pltpu.VMEM((8, 2, 80, 256), F32),
            pltpu.VMEM((2, 2, 2, 80, 256), F32),
            pltpu.VMEM((2, 8, 2, 40, 256), F32),
            pltpu.VMEM((Z, 40, 384), F32),
            pltpu.VMEM((2, 8, 40, 384), F32),
            pltpu.VMEM((2, 8, 40, 384), F32),
            pltpu.VMEM((2, 40, 384), F32),
            dma((4, 9)), dma((4,)), dma((4, 9)),
            dma((2,)),
            dma((2, 3)), dma((2,)),
            dma((3,)), dma((3,)),
            dma((8, 2)), dma((8, 2)),
            dma((3, 2)), dma((3, 2)),
            dma((16,)), dma((2, 8)),
            dma, dma((2, 8, 2)), dma((2, 8, 2)), dma((2,)),
        ],
        compiler_params=pltpu.CompilerParams(collective_id=0, has_side_effects=True),
        name="panel_products",
    )(anc_inverse, panel.T, local_rows.reshape(1, -1))
    sigma_diag = inv_diag - folded
    sigma_off = so.reshape(160, 240).T
    return (sigma_off, sigma_diag)


def solution(mesh):
    placed = (P("row", "col"), P("row", "col"), P("row"), P("row", "col"))
    return jax.shard_map(
        shards,
        mesh=mesh,
        in_specs=placed,
        out_specs=(P("row", "col"), P("row", "col")),
        check_vma=False,
    )
```
